32 devices in a mesh: dp: 16 (over z, y, core), tensor: 2 (over x).
Axes of the slice: x: 2, y: 2, z: 4, core: 2. Of those that a mesh axis runs over, the one named last changes fastest.
Arguments:
- layer_input: float32 [8192, 1024], P(('dp', 'tensor')), may hold values from -6 to 6
- segment_ids: int32 [16, 512], P('dp'), may hold values from 0 to 3, never falling along the last dimension, each value on 1 to 256 neighbouring positions
- norm1_gain: bfloat16 [1024], P('dp'), may hold values from 0.25 to 1.75
- norm1_shift: bfloat16 [1024], P('dp'), may hold values from -3 to 3
- qkv_weight: bfloat16 [1024, 3072], P('dp', 'tensor'), may hold values from -1 to 1
- qkv_bias: bfloat16 [2048], P(('tensor', 'dp')), may hold values from -3 to 3
- dense_weight: bfloat16 [1024, 1024], P('dp', 'tensor'), may hold values from -0.75 to 0.75
- dense_bias: bfloat16 [1024], P('dp'), may hold values from -3 to 3
- norm2_gain: bfloat16 [1024], P('dp'), may hold values from 0.25 to 1.75
- norm2_shift: bfloat16 [1024], P('dp'), may hold values from -3 to 3
- inner_weight: bfloat16 [1024, 4096], P('dp', 'tensor'), may hold values from -0.1875 to 0.1875
- inner_bias: bfloat16 [4096], P(('tensor', 'dp')), may hold values from -3 to 3
- outer_weight: bfloat16 [1024, 4096], P('dp', 'tensor'), may hold values from -0.1875 to 0.1875
- outer_bias: bfloat16 [1024], P('dp'), may hold values from -3 to 3
- out_cotangent: float32 [8192, 1024], P(('dp', 'tensor')), may hold values from -6 to 6
Outputs:
- layer_output: float32 [8192, 1024], P(('dp', 'tensor'))
- input_grad: float32 [8192, 1024], P(('dp', 'tensor'))
- norm1_gain_grad: float32 [1024], P('dp')
- norm1_shift_grad: float32 [1024], P('dp')
- qkv_weight_grad: float32 [1024, 3072], P('dp', 'tensor')
- qkv_bias_grad: float32 [2048], P(('tensor', 'dp'))
- dense_weight_grad: float32 [1024, 1024], P('dp', 'tensor')
- dense_bias_grad: float32 [1024], P('dp')
- norm2_gain_grad: float32 [1024], P('dp')
- norm2_shift_grad: float32 [1024], P('dp')
- inner_weight_grad: float32 [1024, 4096], P('dp', 'tensor')
- inner_bias_grad: float32 [4096], P(('tensor', 'dp'))
- outer_weight_grad: float32 [1024, 4096], P('dp', 'tensor')
- outer_bias_grad: float32 [1024], P('dp')
The draws below stay inside these ranges and needn't reach their ends.
Inputs may be any that keep to these rules, and one draw needn't show every extreme that they name: `segment_ids`: along each row the ids never fall; each segment spans 1 to 256 positions, and one spans exactly 256.
All inputs are finite; a program needn't handle non-finite values.
Results may differ from the reference program's by a relative error of at most 0.024.
Values may be sent and summed in bfloat16 or wider, within the bound.
No kernel may reach another device: no remote copies, remote signals or barrier semaphores. Data moves between devices by JAX's collectives and lax.ppermute only.
A program may use at most 128 MiB of HBM per device.

```python
import math
import jax
import jax.numpy as jnp
import numpy as np
from jax import lax

D = 1024
H = 16
HD = 64
FF = 4096
TOK_DP = 512
SEGS = 4
SEG_MOST = 256
TOKENS = 8192
N_DP = 16
N_TENSOR = 2


def draw_qkv_weight(key, part):
    second_key = jax.random.fold_in(key, 1)
    full = jnp.clip(jax.random.normal(second_key, (D, 3 * D), jnp.float32), -6.0, 6.0)
    return (full * D ** (-0.5)).astype(jnp.bfloat16)


def strengthened(array, key, source, target, parts, factor):
    owner, partner = [(jnp.arange(array.shape[position]) // (array.shape[position] // parts)).reshape([-1 if axis == position else 1 for axis in range(array.ndim)]) for position in (source, target)]
    chosen = jax.random.permutation(key, parts)[partner]
    strong = (owner == chosen) | (owner == (partner + parts // 2) % parts)
    return jnp.where(strong, factor * array, array)


def shard_levels(rng, shape, cuts, low, largest):
    level, own = 1.0, jax.random.fold_in(rng, 6)
    for dim, blocks in cuts:
        steps = jnp.exp(jax.random.uniform(jax.random.fold_in(own, dim), (blocks,), jnp.float32, low / len(cuts), largest / len(cuts)))
        level = level * jnp.repeat(steps, shape[dim] // blocks).reshape([-1 if axis == dim else 1 for axis in range(len(shape))])
    return level


def length_profile(count, total, limit, skew):
    weights = [(1 << 20) // math.isqrt(standing ** skew) + 1 for standing in range(2, count + 1)]
    spare, counts = total - limit - (count - 1), [1] * (count - 1)
    while spare > 0:
        free = [i for i in range(count - 1) if counts[i] < limit]
        pool, left = sum([weights[i] for i in free]), spare
        for i in free:
            addition = min(limit - counts[i], max(1, left * weights[i] // pool), spare)
            counts[i] = counts[i] + addition
            spare = spare - addition
    return np.array([limit] + counts)


def ragged_sizes(stream_key, amount, total, reach, lean):
    if amount == 2:
        one = jax.random.randint(stream_key, (), max(1, total - reach), min(reach, total - 1) + 1)
        return jnp.stack([one, total - one])
    lengths = jnp.asarray(length_profile(amount, total, reach, lean), jnp.int32)
    pairs = (amount - 1) // 2
    source_of, sink = lengths[1:1 + 2 * pairs:2], lengths[2:2 + 2 * pairs:2]
    slack = jnp.minimum(source_of - 1, reach - sink)
    moved = jax.random.randint(jax.random.fold_in(stream_key, 1), (pairs,), 0, 1 << 20) % (slack + 1)
    lengths = lengths.at[1:1 + 2 * pairs:2].set(source_of - moved).at[2:2 + 2 * pairs:2].set(sink + moved)
    return lengths[jax.random.permutation(jax.random.fold_in(stream_key, 2), amount)]


def normal_values(own_key, dims, scale, limit, shards=(), kind=jnp.bfloat16):
    values = jax.random.normal(own_key, dims, jnp.float32) * scale
    if len(shards) > 0:
        values = shard_levels(own_key, dims, shards, -0.22, 0.18) * values
    return jnp.clip(values, min=-limit, max=limit).astype(kind)


def bell_draw_with(own_key, extent, scale, limit, pieces, heavy, held_as=jnp.bfloat16):
    values = scale * jax.random.normal(own_key, extent, jnp.float32)
    if pieces:
        values = values * shard_levels(own_key, extent, pieces, -0.22, 0.18)
    return jnp.clip(strengthened(values, jax.random.fold_in(own_key, 3), *heavy), -limit, limit).astype(held_as)


def setup_inputs(seed: int = 0) -> dict:
    seeds = jax.random.split(jax.random.key(seed), 16)
    return {
        "layer_input": normal_values(seeds[0], (TOKENS, D), 1.0, 6.0, ((0, 32),), jnp.float32),
        "segment_ids": jax.vmap(lambda own: jnp.searchsorted(jnp.cumsum(ragged_sizes(own, SEGS, TOK_DP, SEG_MOST, 2)), jnp.arange(TOK_DP), side="right"))(jax.random.split(seeds[1], N_DP)).reshape((N_DP, TOK_DP)).astype(jnp.int32),
        "norm1_gain": jnp.clip(1.0 + 0.15 * jax.random.normal(seeds[2], (D,), jnp.float32), 0.25, 1.75).astype(jnp.bfloat16),
        "norm1_shift": normal_values(seeds[3], (D,), 0.5, 3.0, ((0, 16),)),
        "qkv_weight": draw_qkv_weight(jax.random.fold_in(seeds[15], 71), 0),
        "qkv_bias": normal_values(seeds[5], (2 * D,), 0.5, 3.0, ((0, 32),)),
        "dense_weight": normal_values(seeds[6], (D, D), HD ** -0.5, 0.75, ((0, 16), (1, 2))),
        "dense_bias": normal_values(seeds[7], (D,), 0.5, 3.0, ((0, 16),)),
        "norm2_gain": jnp.clip(1.0 + 0.15 * jax.random.normal(seeds[8], (D,), jnp.float32), 0.25, 1.75).astype(jnp.bfloat16),
        "norm2_shift": normal_values(seeds[9], (D,), 0.5, 3.0, ((0, 16),)),
        "inner_weight": normal_values(seeds[10], (D, FF), D ** -0.5, 0.1875, ((0, 16), (1, 2))),
        "inner_bias": normal_values(seeds[11], (FF,), 0.5, 3.0, ((0, 32),)),
        "outer_weight": normal_values(seeds[12], (D, FF), (FF // 4) ** -0.5, 0.1875, ((0, 16), (1, 2))),
        "outer_bias": normal_values(seeds[13], (D,), 0.5, 3.0, ((0, 16),)),
        "out_cotangent": bell_draw_with(seeds[14], (TOKENS, D), 1.0, 6.0, ((0, 32),), (0, 1, 32, 2.75), jnp.float32),
    }


EPSILON = 1e-05
GELU_C = 0.7978845608028654
GELU_K = 0.044715

def layer_norm(row_data, gain, shift):
    row_mean = lax.optimization_barrier(jnp.mean(row_data, axis=-1, keepdims=True))
    centered = row_data - row_mean
    row_var = lax.optimization_barrier(jnp.mean(centered * centered, axis=-1, keepdims=True))
    inv_std = lax.rsqrt(row_var + EPSILON)
    normed = centered * inv_std
    return (normed * gain.astype(jnp.float32) + shift.astype(jnp.float32), normed, inv_std)

def norm_back(grad_out, normed, inv_std, gain):
    scaled = grad_out * gain.astype(jnp.float32)
    mean_grad = lax.optimization_barrier(jnp.mean(scaled, axis=-1, keepdims=True))
    mean_cross = lax.optimization_barrier(jnp.mean(scaled * normed, axis=-1, keepdims=True))
    return inv_std * (scaled - mean_grad - normed * mean_cross)

def gelu_parts(pre_act):
    cubed_term = pre_act * pre_act * pre_act
    tangent = jnp.tanh(GELU_C * (pre_act + GELU_K * cubed_term))
    result = 0.5 * pre_act * (1.0 + tangent)
    derivative = 0.5 * (1.0 + tangent) + 0.5 * pre_act * (1.0 - tangent * tangent) * GELU_C * (1.0 + 3.0 * GELU_K * pre_act * pre_act)
    return (result, derivative)

def shard_sum(left, right):
    piece_width = left.shape[1] // N_TENSOR
    total = jnp.zeros((left.shape[0], right.shape[0]), jnp.float32)
    for piece_index in range(N_TENSOR):
        first_col = piece_index * piece_width
        partial_term = lax.dot_general(left[:, first_col:first_col + piece_width], right[:, first_col:first_col + piece_width], (((1,), (1,)), ((), ())), preferred_element_type=jnp.float32)
        rounded = lax.optimization_barrier(partial_term.astype(jnp.bfloat16))
        total = total + rounded.astype(jnp.float32)
    return total

def block_scores(query_block, key_rows, first_row, segment_row, head_slopes):
    block_len = query_block.shape[0]
    scores = jnp.einsum('bhe,the->hbt', query_block.astype(jnp.float32), key_rows.astype(jnp.float32)) * HD ** (-0.5)
    row_pos = first_row + jnp.arange(block_len, dtype=jnp.int32)
    col_pos = jnp.arange(key_rows.shape[0], dtype=jnp.int32)
    segment_query = segment_row[first_row:first_row + block_len]
    allowed = (col_pos[None, :] <= row_pos[:, None]) & (segment_query[:, None] == segment_row[None, :])
    distance = (row_pos[:, None] - col_pos[None, :]).astype(jnp.float32)
    scores = scores - head_slopes[:, None, None] * distance[None]
    return jnp.where(allowed[None], scores, -1e+30)

def attend_forward(query_rows, key_rows, value_rows, segment_row, head_slopes):
    block_len = min(512, query_rows.shape[0])
    outputs = []
    totals = []
    for qblock in range(query_rows.shape[0] // block_len):
        first_row = qblock * block_len
        query_block = query_rows[first_row:first_row + block_len]
        scores = block_scores(query_block, key_rows, first_row, segment_row, head_slopes)
        row_max = lax.optimization_barrier(jnp.max(scores, axis=-1, keepdims=True))
        log_total = row_max + jnp.log(lax.optimization_barrier(jnp.sum(jnp.exp(scores - row_max), axis=-1, keepdims=True)))
        attn_probs = jnp.exp(scores - log_total).astype(jnp.bfloat16)
        context = jnp.einsum('hbt,the->bhe', attn_probs.astype(jnp.float32), value_rows.astype(jnp.float32))
        outputs.append(context.astype(jnp.bfloat16))
        totals.append(log_total)
    return (jnp.concatenate(outputs, axis=0), jnp.concatenate(totals, axis=1))

def attend_backward(query_rows, key_rows, value_rows, context, context_grad, log_total, segment_row, head_slopes):
    block_len = min(512, query_rows.shape[0])
    scale = HD ** (-0.5)
    key_grad = jnp.zeros(key_rows.shape, jnp.float32)
    value_grad = jnp.zeros(value_rows.shape, jnp.float32)
    query_parts = []
    for qblock in range(query_rows.shape[0] // block_len):
        first_row = qblock * block_len
        query_block = query_rows[first_row:first_row + block_len]
        grad_block = context_grad[first_row:first_row + block_len]
        scores = block_scores(query_block, key_rows, first_row, segment_row, head_slopes)
        probs = jnp.exp(scores - log_total[:, first_row:first_row + block_len])
        probs_low = probs.astype(jnp.bfloat16)
        value_grad = value_grad + jnp.einsum('hbt,bhe->the', probs_low.astype(jnp.float32), grad_block.astype(jnp.float32))
        prob_grad = jnp.einsum('bhe,the->hbt', grad_block.astype(jnp.float32), value_rows.astype(jnp.float32))
        delta = lax.optimization_barrier(jnp.sum(grad_block.astype(jnp.float32) * context[first_row:first_row + block_len].astype(jnp.float32), axis=-1))
        score_grad = (probs * (prob_grad - jnp.transpose(delta)[:, :, None])).astype(jnp.bfloat16)
        query_parts.append(jnp.einsum('hbt,the->bhe', score_grad.astype(jnp.float32), key_rows.astype(jnp.float32)) * scale)
        key_grad = key_grad + jnp.einsum('hbt,bhe->the', score_grad.astype(jnp.float32), query_block.astype(jnp.float32)) * scale
    return (jnp.concatenate(query_parts, axis=0), key_grad, value_grad)

def group_pass(weights, layer_rows, cot_rows, segment_row):
    norm1_gain, norm1_shift, qkv_weight, qkv_bias, dense_weight, dense_bias, norm2_gain, norm2_shift, inner_weight, inner_bias, outer_weight, outer_bias = weights
    row_count = layer_rows.shape[0]
    head_slopes = jnp.exp2(-8.0 * (jnp.arange(H).astype(jnp.float32) + 1.0) / H)
    bias_pairs = qkv_bias.astype(jnp.float32).reshape(H, 2, HD)
    bias_three = jnp.stack([bias_pairs[:, 0], jnp.zeros_like(bias_pairs[:, 0]), bias_pairs[:, 1]], axis=1).reshape(-1)
    normed_one, hat_one, inv_one = layer_norm(layer_rows, norm1_gain, norm1_shift)
    norm_low = normed_one.astype(jnp.bfloat16)
    projected = (jnp.dot(norm_low, qkv_weight, preferred_element_type=jnp.float32) + bias_three).astype(jnp.bfloat16)
    projected = projected.reshape(row_count, H, 3, HD)
    query_rows = projected[:, :, 0]
    key_rows = projected[:, :, 1]
    value_rows = projected[:, :, 2]
    context, log_total = attend_forward(query_rows, key_rows, value_rows, segment_row, head_slopes)
    context_flat = context.reshape(row_count, D)
    middle = layer_rows + shard_sum(context_flat, dense_weight) + dense_bias.astype(jnp.float32)
    normed_two, hat_two, inv_two = layer_norm(middle, norm2_gain, norm2_shift)
    mid_low = normed_two.astype(jnp.bfloat16)
    pre_act = jnp.dot(mid_low, inner_weight, preferred_element_type=jnp.float32) + inner_bias.astype(jnp.float32)
    act_value, act_slope = gelu_parts(pre_act)
    act_low = act_value.astype(jnp.bfloat16)
    layer_output = middle + shard_sum(act_low, outer_weight) + outer_bias.astype(jnp.float32)
    cot_low = cot_rows.astype(jnp.bfloat16)
    outer_grad = jnp.dot(cot_low.T, act_low, preferred_element_type=jnp.float32)
    outer_bias_grad = lax.optimization_barrier(jnp.sum(cot_rows, axis=0))
    pre_grad = jnp.dot(cot_low, outer_weight, preferred_element_type=jnp.float32) * act_slope
    inner_bias_grad = lax.optimization_barrier(jnp.sum(pre_grad, axis=0))
    pre_low = pre_grad.astype(jnp.bfloat16)
    inner_grad = jnp.dot(mid_low.T, pre_low, preferred_element_type=jnp.float32)
    mid_grad = shard_sum(pre_low, inner_weight)
    gain_two_grad = lax.optimization_barrier(jnp.sum(mid_grad * hat_two, axis=0))
    shift_two_grad = lax.optimization_barrier(jnp.sum(mid_grad, axis=0))
    middle_grad = cot_rows + norm_back(mid_grad, hat_two, inv_two, norm2_gain)
    dense_bias_grad = lax.optimization_barrier(jnp.sum(middle_grad, axis=0))
    middle_low = middle_grad.astype(jnp.bfloat16)
    dense_grad = jnp.dot(middle_low.T, context_flat, preferred_element_type=jnp.float32)
    context_grad = jnp.dot(middle_low, dense_weight, preferred_element_type=jnp.float32).astype(jnp.bfloat16)
    context_grad = context_grad.reshape(row_count, H, HD)
    query_grad, key_grad, value_grad = attend_backward(query_rows, key_rows, value_rows, context, context_grad, log_total, segment_row, head_slopes)
    qkv_grad = jnp.stack([query_grad, key_grad, value_grad], axis=2).reshape(row_count, 3 * D)
    bias_sums = lax.optimization_barrier(jnp.sum(qkv_grad, axis=0)).reshape(H, 3, HD)
    qkv_bias_grad = jnp.stack([bias_sums[:, 0], bias_sums[:, 2]], axis=1).reshape(-1)
    qkv_low = qkv_grad.astype(jnp.bfloat16)
    qkv_weight_grad = jnp.dot(norm_low.T, qkv_low, preferred_element_type=jnp.float32)
    first_grad = shard_sum(qkv_low, qkv_weight)
    gain_one_grad = lax.optimization_barrier(jnp.sum(first_grad * hat_one, axis=0))
    shift_one_grad = lax.optimization_barrier(jnp.sum(first_grad, axis=0))
    input_grad = middle_grad + norm_back(first_grad, hat_one, inv_one, norm1_gain)
    grads = (gain_one_grad, shift_one_grad, qkv_weight_grad, qkv_bias_grad, dense_grad, dense_bias_grad, gain_two_grad, shift_two_grad, inner_grad, inner_bias_grad, outer_grad, outer_bias_grad)
    return (grads, (layer_output, input_grad))

def reference(layer_input, segment_ids, norm1_gain, norm1_shift, qkv_weight, qkv_bias, dense_weight, dense_bias, norm2_gain, norm2_shift, inner_weight, inner_bias, outer_weight, outer_bias, out_cotangent):
    weights = (norm1_gain, norm1_shift, qkv_weight, qkv_bias, dense_weight, dense_bias, norm2_gain, norm2_shift, inner_weight, inner_bias, outer_weight, outer_bias)
    input_groups = layer_input.reshape(N_DP, TOK_DP, D)
    cot_groups = out_cotangent.reshape(N_DP, TOK_DP, D)
    zero_grads = tuple((jnp.zeros(weight.shape, jnp.float32) for weight in weights))

    def group_step(running, inputs):
        grads, outputs = group_pass(weights, inputs[0], inputs[1], inputs[2])
        return (tuple((left + right for left, right in zip(running, grads))), outputs)
    totals, (output_groups, grad_groups) = lax.scan(group_step, zero_grads, (input_groups, cot_groups, segment_ids))
    return (output_groups.reshape(TOKENS, D), grad_groups.reshape(TOKENS, D), totals[0], totals[1], totals[2], totals[3], totals[4], totals[5], totals[6], totals[7], totals[8], totals[9], totals[10], totals[11])
```

```python
import jax
import jax.numpy as jnp
import numpy as np
from jax import lax
from jax.experimental import pallas as pl
from jax.experimental.pallas import tpu as pltpu
from jax.sharding import PartitionSpec as P

H = 16
HD = 64
EPSILON = 1e-05
GELU_C = 0.7978845608028654
GELU_K = 0.044715
F32 = jnp.float32
LOW = jnp.bfloat16


class Ring:
    def __init__(self, n_dp):
        self.n_dp = n_dp
        chips = n_dp // 2
        depth = chips // 2
        order = [2 * z for z in range(depth)] + [2 * z + 1 for z in reversed(range(depth))]
        self.n_fwd = chips // 2
        self.n_bwd = chips - 1 - self.n_fwd
        self.fwd = []
        for k in range(chips):
            self.fwd.append((2 * order[k], 2 * order[(k + 1) % chips]))
            self.fwd.append((2 * order[k] + 1, 2 * order[k - 1] + 1))
        self.bwd = [(b, a) for a, b in self.fwd]
        self.core = [(i, i ^ 1) for i in range(n_dp)]
        lists = {}
        for k in range(chips):
            for core, sign in ((0, 1), (1, -1)):
                steps = [0] + [-s for s in range(1, self.n_fwd + 1)] + list(range(1, self.n_bwd + 1))
                lists[2 * order[k] + core] = [2 * order[(k + sign * s) % chips] + core for s in steps]
        self.table = np.array([lists[i] + lists[i ^ 1] for i in range(n_dp)], np.int32)
        self.inverse = np.argsort(self.table, axis=1).astype(np.int32)

    def gather(self, shard):
        ahead, behind = [shard], [shard]
        for step in range(self.n_fwd):
            ahead.append(lax.ppermute(ahead[-1], "dp", self.fwd))
            if step < self.n_bwd:
                behind.append(lax.ppermute(behind[-1], "dp", self.bwd))
        own = ahead + behind[1:]
        late = [self.n_fwd - 1, self.n_fwd, self.n_fwd + self.n_bwd]
        early = [j for j in range(len(own)) if j not in late]
        rows = shard.shape[0]
        first = lax.ppermute(jnp.concatenate([own[j] for j in early]), "dp", self.core)
        second = lax.ppermute(jnp.concatenate([own[j] for j in late]), "dp", self.core)
        other = [None] * len(own)
        for place, j in enumerate(early):
            other[j] = first[place * rows : (place + 1) * rows]
        for place, j in enumerate(late):
            other[j] = second[place * rows : (place + 1) * rows]
        return own + other

    def scatter(self, own_half, other_half):
        came = lax.ppermute(other_half, "dp", self.core)
        rows = own_half.shape[0] // (self.n_dp // 2)

        def block(j):
            part = slice(j * rows, (j + 1) * rows)
            return own_half[part].astype(F32) + came[part].astype(F32)

        ahead = lax.ppermute(block(self.n_fwd).astype(LOW), "dp", self.fwd)
        behind = lax.ppermute(block(self.n_bwd).astype(LOW), "dp", self.bwd)
        for step in range(1, self.n_fwd):
            distance = self.n_fwd - step
            term = block(self.n_fwd + distance)
            ahead = lax.ppermute((ahead.astype(F32) + term).astype(LOW), "dp", self.fwd)
            distance = self.n_bwd - step
            if distance >= 1:
                behind = lax.ppermute(
                    (behind.astype(F32) + block(distance)).astype(LOW), "dp", self.bwd
                )
        return ahead.astype(F32) + behind.astype(F32) + block(0)

    def total(self, values):
        step = 1
        while step < self.n_dp:
            values = values + lax.ppermute(values, "dp", [(i, i ^ step) for i in range(self.n_dp)])
            step *= 2
        return values


def move_blocks_kernel(source, x_ref, o_ref):
    lane = lax.broadcasted_iota(jnp.int32, (x_ref.shape[0], 128), 1)
    for tile in range(x_ref.shape[1] // 128):
        halves = []
        for half in range(2):
            block = source[2 * tile + half]
            start = pl.multiple_of(lax.shift_right_logical(block, 1) * 128, 128)
            taken = x_ref[:, pl.ds(start, 128)]
            moved = pltpu.roll(taken, 64, 1)
            halves.append(jnp.where((block & 1) == half, taken, moved))
        o_ref[:, tile * 128 : (tile + 1) * 128] = jnp.where(lane < 64, halves[0], halves[1])


def move_blocks(x, source):
    count = source.shape[0]
    rows, width = x.shape
    if width // count != 64:
        return jnp.take(x.reshape(rows, count, width // count), source, axis=1).reshape(rows, width)
    tall = min(rows, 256)
    return pl.pallas_call(
        move_blocks_kernel,
        out_shape=jax.ShapeDtypeStruct(x.shape, x.dtype),
        grid_spec=pltpu.PrefetchScalarGridSpec(
            num_scalar_prefetch=1,
            grid=(rows // tall,),
            in_specs=[pl.BlockSpec((tall, width), lambda i, s: (i, 0))],
            out_specs=pl.BlockSpec((tall, width), lambda i, s: (i, 0)),
        ),
        name="move_blocks",
    )(source, x)


def norm_stats(rows):
    mean = jnp.mean(rows, axis=-1, keepdims=True)
    centered = rows - mean
    inv = lax.rsqrt(jnp.mean(centered * centered, axis=-1, keepdims=True) + EPSILON)
    return centered * inv, inv


def norm_back(grad_out, normed, inv_std, gain):
    scaled = grad_out * gain
    mean_grad = jnp.mean(scaled, axis=-1, keepdims=True)
    mean_cross = jnp.mean(scaled * normed, axis=-1, keepdims=True)
    return inv_std * (scaled - mean_grad - normed * mean_cross)


def gelu_parts(pre_act):
    cubed_term = pre_act * pre_act * pre_act
    tangent = jnp.tanh(GELU_C * (pre_act + GELU_K * cubed_term))
    result = 0.5 * pre_act * (1.0 + tangent)
    derivative = 0.5 * (1.0 + tangent) + 0.5 * pre_act * (1.0 - tangent * tangent) * GELU_C * (
        1.0 + 3.0 * GELU_K * pre_act * pre_act
    )
    return (result, derivative)


def plain_product(left, right):
    return jnp.dot(left, right, preferred_element_type=F32)


def rows_product(left, right):
    return lax.dot_general(left, right, (((0,), (0,)), ((), ())), preferred_element_type=F32)


def cross_product(left, right):
    return lax.dot_general(left, right, (((1,), (1,)), ((), ())), preferred_element_type=F32)


def block_scores(query_rows, key_rows, segment_row, position, head_slopes):
    scores = jnp.einsum("bhe,the->hbt", query_rows, key_rows, preferred_element_type=F32)
    scores = scores * HD ** (-0.5)
    allowed = (position[None, :] <= position[:, None]) & (
        segment_row[:, None] == segment_row[None, :]
    )
    distance = (position[:, None] - position[None, :]).astype(F32)
    scores = scores - head_slopes[:, None, None] * distance[None]
    return jnp.where(allowed[None], scores, -1e30)


def attend_forward(query_rows, key_rows, value_rows, segment_row, position, head_slopes):
    scores = block_scores(query_rows, key_rows, segment_row, position, head_slopes)
    row_max = jnp.max(scores, axis=-1, keepdims=True)
    log_total = row_max + jnp.log(jnp.sum(jnp.exp(scores - row_max), axis=-1, keepdims=True))
    attn_probs = jnp.exp(scores - log_total).astype(LOW)
    context = jnp.einsum("hbt,the->bhe", attn_probs, value_rows, preferred_element_type=F32)
    return context.astype(LOW), log_total


def attend_backward(
    query_rows, key_rows, value_rows, context, context_grad, log_total, segment_row, position, slopes
):
    scale = HD ** (-0.5)
    scores = block_scores(query_rows, key_rows, segment_row, position, slopes)
    probs = jnp.exp(scores - log_total)
    probs_low = probs.astype(LOW)
    value_grad = jnp.einsum("hbt,bhe->the", probs_low, context_grad, preferred_element_type=F32)
    prob_grad = jnp.einsum("bhe,the->hbt", context_grad, value_rows, preferred_element_type=F32)
    delta = jnp.sum(context_grad.astype(F32) * context.astype(F32), axis=-1)
    score_grad = (probs * (prob_grad - jnp.transpose(delta)[:, :, None])).astype(LOW)
    query_grad = (
        jnp.einsum("hbt,the->bhe", score_grad, key_rows, preferred_element_type=F32) * scale
    )
    key_grad = jnp.einsum("hbt,bhe->the", score_grad, query_rows, preferred_element_type=F32) * scale
    return query_grad, key_grad, value_grad


def on_device(n_dp, n_tensor, *args):
    (
        layer_input,
        segment_ids,
        norm1_gain,
        norm1_shift,
        qkv_weight,
        qkv_bias,
        dense_weight,
        dense_bias,
        norm2_gain,
        norm2_shift,
        inner_weight,
        inner_bias,
        outer_weight,
        outer_bias,
        out_cotangent,
    ) = args
    ring = Ring(n_dp)
    own_rows, width = layer_input.shape
    rows = own_rows * n_tensor
    block = width // n_dp
    half = width // 2
    me = lax.axis_index("dp")
    side = lax.axis_index("tensor")
    order = jnp.asarray(ring.table)[me]
    inverse = jnp.asarray(ring.inverse)[me]
    swap = [(0, 1), (1, 0)]

    def all_rows(mine):
        if n_tensor == 2:
            return [mine, lax.ppermute(mine, "tensor", swap)]
        gathered = lax.all_gather(mine, "tensor", axis=0, tiled=True)
        return [gathered[i * own_rows : (i + 1) * own_rows] for i in range(n_tensor)]

    def sum_to_own(term):
        if n_tensor == 2:
            sent = lax.ppermute(term(1).astype(LOW), "tensor", swap)
            return sent.astype(F32) + term(0).astype(LOW).astype(F32)
        return lax.psum_scatter(
            jnp.concatenate([term(i) for i in range(n_tensor)]).astype(LOW),
            "tensor",
            scatter_dimension=0,
            tiled=True,
        ).astype(F32)

    position = jnp.arange(rows, dtype=jnp.int32)
    segment_row = segment_ids[0]
    if n_tensor == 2:
        position = (position + side * own_rows) % rows
        turned = jnp.concatenate([segment_row[own_rows:], segment_row[:own_rows]])
        segment_row = jnp.where(side == 0, segment_row, turned)

    small = [norm1_gain, norm1_shift, dense_bias, norm2_gain, norm2_shift, outer_bias]
    small = jnp.concatenate(small + [qkv_bias, inner_bias])
    n_small, n_qkv_bias = small.shape[0], qkv_bias.shape[0]
    small = jnp.pad(small, (0, block * 128 - n_small)).reshape(block, 128)
    qkv_cols, dense_cols = qkv_weight.shape[1], dense_weight.shape[1]
    first_set = ring.gather(jnp.concatenate([qkv_weight, small], axis=1))
    qkv_full = jnp.concatenate([b[:, :qkv_cols] for b in first_set])
    used = -(-n_small // 128)
    small_full = jnp.stack([b[:used, qkv_cols:].reshape(-1) for b in first_set]).astype(F32)
    vectors = [small_full[:, i * block : (i + 1) * block].reshape(-1) for i in range(6)]
    gain_one, shift_one, dense_bias_full, gain_two, shift_two, outer_bias_full = vectors
    bias_blocks = small_full[:, 6 * block : n_small][inverse]
    qkv_bias_full = bias_blocks[:, :n_qkv_bias].reshape(-1)
    inner_bias_full = bias_blocks[:, n_qkv_bias:].reshape(-1)

    second_set = ring.gather(jnp.concatenate([dense_weight, inner_weight], axis=1))
    dense_full = jnp.concatenate([b[:, :dense_cols] for b in second_set])
    inner_full = jnp.concatenate([b[:, dense_cols:] for b in second_set])
    outer_full = jnp.concatenate(ring.gather(outer_weight))

    local_heads = qkv_cols // (3 * HD)
    head_index = side * local_heads + jnp.arange(local_heads, dtype=jnp.int32)
    head_slopes = jnp.exp2(-8.0 * (head_index.astype(F32) + 1.0) / H)
    bias_pairs = qkv_bias_full.reshape(local_heads, 2, HD)
    bias_three = jnp.stack(
        [bias_pairs[:, 0], jnp.zeros_like(bias_pairs[:, 0]), bias_pairs[:, 1]], axis=1
    ).reshape(-1)

    residual = move_blocks(layer_input, order)
    cot_own = move_blocks(out_cotangent, order)
    cot_low = all_rows(cot_own.astype(LOW))
    cot_rows = jnp.concatenate(cot_low)

    hat_one, inv_one = norm_stats(residual)
    hat_rows = jnp.concatenate(all_rows(hat_one.astype(LOW)))
    norm_rows = (hat_rows.astype(F32) * gain_one + shift_one).astype(LOW)
    projected = (plain_product(norm_rows, qkv_full) + bias_three).astype(LOW)
    projected = projected.reshape(rows, local_heads, 3, HD)
    query_rows = projected[:, :, 0]
    key_rows = projected[:, :, 1]
    value_rows = projected[:, :, 2]
    context, log_total = attend_forward(
        query_rows, key_rows, value_rows, segment_row, position, head_slopes
    )
    context_flat = context.reshape(rows, local_heads * HD)

    def part(array, i):
        return array[i * own_rows : (i + 1) * own_rows]

    attn_part = sum_to_own(lambda i: cross_product(part(context_flat, i), dense_full))
    middle = residual + attn_part + dense_bias_full
    hat_two, inv_two = norm_stats(middle)
    mid_list = all_rows((hat_two * gain_two + shift_two).astype(LOW))
    mid_rows = jnp.concatenate(mid_list)
    act_low, slope = [], []
    for mid_part in mid_list:
        value, derivative = gelu_parts(plain_product(mid_part, inner_full) + inner_bias_full)
        act_low.append(value.astype(LOW))
        slope.append(derivative)
    pre_grad = [plain_product(c, outer_full) * s for c, s in zip(cot_low, slope)]
    inner_bias_grad = sum(jnp.sum(g, axis=0) for g in pre_grad)
    pre_low = [g.astype(LOW) for g in pre_grad]
    mid_grad = sum_to_own(lambda i: cross_product(pre_low[i], inner_full))
    act_rows, pre_rows = jnp.concatenate(act_low), jnp.concatenate(pre_low)

    def weight_grad(left, right):
        other = rows_product(left[:, half:], right).astype(LOW)
        own = rows_product(left[:, :half], right).astype(LOW)
        return ring.scatter(own, other)

    outer_grad = weight_grad(cot_rows, act_rows)
    inner_grad = weight_grad(mid_rows, pre_rows)

    ffn_part = sum_to_own(lambda i: cross_product(act_low[i], outer_full))
    layer_output = move_blocks(middle + ffn_part + outer_bias_full, inverse)

    gain_two_grad = jnp.sum(mid_grad * hat_two, axis=0)
    shift_two_grad = jnp.sum(mid_grad, axis=0)
    middle_grad = cot_own + norm_back(mid_grad, hat_two, inv_two, gain_two)
    dense_bias_grad = jnp.sum(middle_grad, axis=0)
    outer_bias_grad = jnp.sum(cot_own, axis=0)
    middle_rows = jnp.concatenate(all_rows(middle_grad.astype(LOW)))
    context_grad = plain_product(middle_rows, dense_full).astype(LOW)
    context_grad = context_grad.reshape(rows, local_heads, HD)
    query_grad, key_grad, value_grad = attend_backward(
        query_rows,
        key_rows,
        value_rows,
        context,
        context_grad,
        log_total,
        segment_row,
        position,
        head_slopes,
    )
    qkv_grad = jnp.stack([query_grad, key_grad, value_grad], axis=2).reshape(rows, qkv_cols)
    bias_sums = jnp.sum(qkv_grad, axis=0).reshape(local_heads, 3, HD)
    qkv_bias_grad = jnp.stack([bias_sums[:, 0], bias_sums[:, 2]], axis=1).reshape(-1)
    qkv_low = qkv_grad.astype(LOW)
    first_grad = sum_to_own(lambda i: cross_product(part(qkv_low, i), qkv_full))
    dense_grad = weight_grad(middle_rows, context_flat)
    qkv_weight_grad = weight_grad(norm_rows, qkv_low)
    gain_one_grad = jnp.sum(first_grad * hat_one, axis=0)
    shift_one_grad = jnp.sum(first_grad, axis=0)
    input_grad = middle_grad + norm_back(first_grad, hat_one, inv_one, gain_one)
    input_grad = move_blocks(input_grad, inverse)

    over_rows = jnp.stack(
        [
            gain_one_grad,
            shift_one_grad,
            dense_bias_grad,
            gain_two_grad,
            shift_two_grad,
            outer_bias_grad,
        ]
    )
    if n_tensor == 2:
        over_rows = over_rows + lax.ppermute(over_rows, "tensor", swap)
    else:
        over_rows = lax.psum(over_rows, "tensor")
    over_rows = over_rows.reshape(6, n_dp, block)[:, inverse]
    small_grads = jnp.concatenate(
        [
            jnp.transpose(over_rows, (1, 0, 2)).reshape(n_dp, 6 * block),
            qkv_bias_grad.reshape(n_dp, -1),
            inner_bias_grad.reshape(n_dp, -1),
        ],
        axis=1,
    )
    mine = lax.dynamic_index_in_dim(ring.total(small_grads), me, axis=0, keepdims=False)
    cut = [mine[i * block : (i + 1) * block] for i in range(6)]
    end = 6 * block + qkv_bias.shape[0]
    return (
        layer_output,
        input_grad,
        cut[0],
        cut[1],
        qkv_weight_grad,
        mine[6 * block : end],
        dense_grad,
        cut[2],
        cut[3],
        cut[4],
        inner_grad,
        mine[end:],
        outer_grad,
        cut[5],
    )


def solution(mesh):
    weight = P("dp", "tensor")
    vector = P("dp")
    columns = P(("tensor", "dp"))
    stream = P(("dp", "tensor"), None)
    in_specs = (
        stream,
        P("dp", None),
        vector,
        vector,
        weight,
        columns,
        weight,
        vector,
        vector,
        vector,
        weight,
        columns,
        weight,
        vector,
        stream,
    )
    out_specs = (
        stream,
        stream,
        vector,
        vector,
        weight,
        columns,
        weight,
        vector,
        vector,
        vector,
        weight,
        columns,
        weight,
        vector,
    )
    n_dp, n_tensor = mesh.shape["dp"], mesh.shape["tensor"]

    def body(*args):
        return on_device(n_dp, n_tensor, *args)

    return jax.shard_map(body, mesh=mesh, in_specs=in_specs, out_specs=out_specs, check_vma=False)
```
